32 devices in a mesh: tm: 4 (over x, core), chan: 8 (over z, y).
Axes of the slice: x: 2, y: 2, z: 4, core: 2. Of those that a mesh axis runs over, the one named last changes fastest.
Arguments:
- raw: bfloat16 [512, 131072], P('chan', 'tm'), may hold values from -6 to 6
- starts: int32 [32], P('tm'), may hold values from 0 to 28672
- dead_mask: int32 [512], P('chan'), may hold values 0 or 1
- offsets: int32 [16], replicated, may hold values from 1 to 256, as said below
Outputs:
- correlations: float32 [16, 512, 256], P('tm', 'chan')
The draws below stay inside these ranges and needn't reach their ends.
Inputs may be any that keep to these rules, and one draw needn't show every extreme that they name: `offsets`: the entries are distinct, and 256 is always one of them.
All inputs are finite; a program needn't handle non-finite values. No bound on the sum of `dead_mask` on one device may be relied on, other than what follows from the above.
Results may differ from the reference program's by a relative error of at most 0.0049.
Values may be sent and summed in bfloat16 or wider, within the bound.
A program may use at most 128 MiB of HBM per device.

```python
import jax
import jax.numpy as jnp
from jax import lax

W_DEV = 8
HOP = 4096
F = 640
F0 = 16
LAGS = 256
MAXOFF = 256
NOFF = 16
WIN = 8192
CH = 512
WINDOWS = 32
SAMPLES = 131072


def draw_offsets(key, part):
    chosen = jax.random.permutation(jax.random.fold_in(key, 11), MAXOFF - 1).astype(jnp.int32) + 1
    values = jnp.concatenate([chosen[:NOFF - 1], jnp.full((1,), MAXOFF, jnp.int32)])
    order = jax.random.permutation(jax.random.fold_in(key, 23), NOFF)
    return values[order].astype(jnp.int32)


def touch_ends(drawn, key, low, top_value):
    index_at = [jax.random.randint(jax.random.fold_in(key, axis), (), 0, length) for axis, length in enumerate(drawn.shape)]
    longest = drawn.shape.index(max(drawn.shape))
    neighbour = index_at[:longest] + [(index_at[longest] + 1) % drawn.shape[longest]] + index_at[longest + 1:]
    return drawn.at[tuple(index_at)].set(low).at[tuple(neighbour)].set(top_value)


def block_scale(key, extent, shards, low, high):
    gain = 1.0
    for position, shards_of in shards:
        steps = jax.random.uniform(jax.random.fold_in(jax.random.fold_in(key, 6), position), (shards_of,), jnp.float32, low / len(shards), high / len(shards))
        gain = gain * jnp.repeat(jnp.exp(steps), extent[position] // shards_of).reshape((-1,) + (1,) * (len(extent) - 1 - position))
    return gain


def bell_draw(stream_key, shape, deviation, bound, shards=(), held_as=jnp.bfloat16):
    result = deviation * jax.random.normal(stream_key, shape, jnp.float32)
    if shards:
        result = result * block_scale(stream_key, shape, shards, -0.22, 0.18)
    return jnp.clip(result, -bound, bound).astype(held_as)


def setup_inputs(seed: int = 0) -> dict:
    key_of = jax.random.split(jax.random.key(seed), 5)
    return {
        "raw": bell_draw(key_of[0], (CH, SAMPLES), 1.0, 6.0, ((0, 8), (1, 4))),
        "starts": touch_ends(jax.random.randint(key_of[1], (WINDOWS,), 0, (W_DEV - 1) * HOP + 1), jax.random.fold_in(key_of[1], 1), 0, (W_DEV - 1) * HOP).astype(jnp.int32),
        "dead_mask": touch_ends((jax.random.randint(key_of[2], (CH,), 0, 8) < 7).astype(jnp.int32), jax.random.fold_in(key_of[2], 1), 0, 1),
        "offsets": draw_offsets(jax.random.fold_in(key_of[4], 71), 0),
    }


def forward_table(first, count):
    sample = jnp.arange(count, dtype=jnp.int32) + first
    bins = jnp.arange(F, dtype=jnp.int32) + F0
    phase = sample[:, None] * bins[None, :] % WIN
    angle = 2.0 * jnp.pi / WIN * phase.astype(jnp.float32)
    return jnp.concatenate([jnp.cos(angle), -jnp.sin(angle)], axis=1).astype(jnp.bfloat16)

def inverse_table():
    bins = jnp.arange(F, dtype=jnp.int32) + F0
    lagged = jnp.arange(LAGS, dtype=jnp.int32) - LAGS // 2
    phase = jnp.mod(bins[:, None] * lagged[None, :], WIN)
    angle = 2.0 * jnp.pi / WIN * phase.astype(jnp.float32)
    return jnp.concatenate([jnp.cos(angle), -jnp.sin(angle)], axis=0)

def whiten(spectrum, live):
    real_part = spectrum[..., :F]
    imag_part = spectrum[..., F:]
    amplitude = jnp.sqrt(real_part * real_part + imag_part * imag_part)
    level = lax.optimization_barrier(jnp.mean(amplitude, axis=-1, keepdims=True))
    scaled = 1.0 / (amplitude + 0.1 * level + 1e-06)
    scaled = jnp.concatenate([scaled, scaled], axis=-1)
    return (spectrum * scaled * live[:, None]).astype(jnp.bfloat16)

def reference(raw, starts, dead_mask, offsets):
    padded = jnp.concatenate([raw, jnp.zeros((CH, HOP), jnp.bfloat16)], axis=1)
    group = jnp.arange(WINDOWS, dtype=jnp.int32) // W_DEV
    begin = (group * (W_DEV * HOP) + starts).astype(jnp.int32)
    hann = 0.5 - 0.5 * jnp.cos(2.0 * jnp.pi * jnp.arange(WIN, dtype=jnp.float32) / WIN)
    table = forward_table(0, WIN)
    live = dead_mask.astype(jnp.float32)

    def one_window(first):
        segment = lax.dynamic_slice_in_dim(padded, first, WIN, 1)
        tapered = (segment.astype(jnp.float32) * hann[None, :]).astype(jnp.bfloat16)
        spectrum = jnp.dot(tapered, table, preferred_element_type=jnp.float32)
        return whiten(spectrum, live)
    white = lax.map(one_window, begin)
    extended = jnp.concatenate([white, jnp.zeros((WINDOWS, MAXOFF, 2 * F), jnp.bfloat16)], axis=1)
    back = inverse_table()
    scale = 1.0 / jnp.sqrt(jnp.float32(WINDOWS * F))
    own = white.astype(jnp.float32)

    def one_offset(distance):
        partner = lax.dynamic_slice_in_dim(extended, distance.astype(jnp.int32), CH, 1).astype(jnp.float32)
        a_re, a_im = (own[..., :F], own[..., F:])
        b_re, b_im = (partner[..., :F], partner[..., F:])
        stack_re = lax.optimization_barrier(jnp.sum(a_re * b_re + a_im * b_im, axis=0))
        stack_im = lax.optimization_barrier(jnp.sum(a_im * b_re - a_re * b_im, axis=0))
        stack = jnp.concatenate([stack_re, stack_im], axis=1)
        return jnp.dot(stack, back, precision=lax.Precision.HIGHEST, preferred_element_type=jnp.float32) * scale
    return lax.map(one_offset, offsets)
```

```python
import functools

import jax
import jax.numpy as jnp
from jax import lax
from jax.experimental import pallas as pl
from jax.experimental.pallas import tpu as pltpu
from jax.sharding import PartitionSpec as P

HOP = 4096
F = 640
F0 = 16
LAGS = 256
MAXOFF = 256
LANES = 128
BLOCK = 512
FINE = 64
MESH = pl.DeviceIdType.MESH


def shifted(block, axis, distance):
    devices = range(lax.axis_size(axis))
    route = [(i - distance, i) for i in devices if i - distance in devices]
    return lax.ppermute(block, axis, route)


def waves(samples):
    bins = jnp.arange(F, dtype=jnp.int32) + F0
    phase = samples[:, None] * bins[None, :] % (2 * HOP)
    angle = 2.0 * jnp.pi / (2 * HOP) * phase.astype(jnp.float32)
    return jnp.cos(angle), jnp.sin(angle)


def base_table():
    fine_c, fine_s = waves(jnp.arange(FINE, dtype=jnp.int32))
    wide_c, wide_s = waves(jnp.arange(BLOCK // FINE, dtype=jnp.int32) * FINE)
    fine_c, fine_s = fine_c[None], fine_s[None]
    wide_c, wide_s = wide_c[:, None], wide_s[:, None]
    cosines = wide_c * fine_c - wide_s * fine_s
    sines = wide_s * fine_c + wide_c * fine_s
    return cosines.reshape(BLOCK, F), sines.reshape(BLOCK, F)


def inverse_table():
    bins = jnp.arange(F, dtype=jnp.int32) + F0
    lagged = jnp.arange(LAGS, dtype=jnp.int32) - LAGS // 2
    phase = jnp.mod(bins[:, None] * lagged[None, :], 2 * HOP)
    angle = 2.0 * jnp.pi / (2 * HOP) * phase.astype(jnp.float32)
    return jnp.concatenate([jnp.cos(angle), -jnp.sin(angle)], axis=0)


def spectra_kernel(
    starts, raw, halo, base_c, base_s, turn_c, turn_s, hann, live, white, pad, tap, table, acc, sems
):
    rows, length = raw.shape
    window_count = starts.shape[0]
    first = pltpu.make_async_copy(raw, pad.at[:, pl.ds(0, length)], sems.at[0])
    second = pltpu.make_async_copy(halo, pad.at[:, pl.ds(length, HOP)], sems.at[1])
    first.start()
    second.start()
    acc[...] = jnp.zeros_like(acc)
    lane = lax.broadcasted_iota(jnp.int32, (rows, LANES), 1)
    first.wait()
    second.wait()

    def step(number, carry):
        ct, st = turn_c[number], turn_s[number]
        bc, bs = base_c[...], base_s[...]
        table[:, :F] = (bc * ct - bs * st).astype(jnp.bfloat16)
        table[:, F:] = (-(bs * ct + bc * st)).astype(jnp.bfloat16)
        taper = hann[number]
        for w in range(window_count):
            begin = starts[w]
            rest = lax.rem(begin, LANES)
            column = pl.multiple_of(begin - rest + number * BLOCK, LANES)
            turn = lax.rem(LANES - rest, LANES)
            keep = lane < LANES - rest
            rolled = None
            for j in range(BLOCK // LANES + 1):
                piece = pad[:, pl.ds(pl.multiple_of(column + j * LANES, LANES), LANES)]
                following = pltpu.roll(piece.astype(jnp.float32), turn, 1)
                if j:
                    lo = (j - 1) * LANES
                    value = jnp.where(keep, rolled, following) * taper[:, lo : lo + LANES]
                    tap[w * rows : (w + 1) * rows, lo : lo + LANES] = value.astype(jnp.bfloat16)
                rolled = following
        acc[...] += jnp.dot(tap[...], table[...], preferred_element_type=jnp.float32)
        return carry

    lax.fori_loop(0, 2 * HOP // BLOCK, step, 0)

    def whiten(w, carry):
        at = pl.ds(pl.multiple_of(w * rows, rows), rows)
        real_part = acc[at, :F]
        imag_part = acc[at, F:]
        amplitude = jnp.sqrt(real_part * real_part + imag_part * imag_part)
        level = jnp.mean(amplitude, axis=-1, keepdims=True)
        scaled = live[...] / (amplitude + 0.1 * level + 1e-06)
        white[w, :, :F] = (real_part * scaled).astype(jnp.bfloat16)
        white[w, :, F:] = (imag_part * scaled).astype(jnp.bfloat16)
        return carry

    lax.fori_loop(0, window_count, whiten, 0)


def spectra(raw, halo, starts, live):
    rows, length = raw.shape
    window_count = starts.shape[0]
    blocks = 2 * HOP // BLOCK
    base_c, base_s = base_table()
    turn_c, turn_s = waves(jnp.arange(blocks, dtype=jnp.int32) * BLOCK)
    sample = jnp.arange(2 * HOP, dtype=jnp.float32)
    hann = 0.5 - 0.5 * jnp.cos(2.0 * jnp.pi * sample / (2 * HOP))
    vmem = pl.BlockSpec(memory_space=pltpu.VMEM)
    hbm = pl.BlockSpec(memory_space=pl.ANY)
    total = window_count * rows
    return pl.pallas_call(
        spectra_kernel,
        out_shape=jax.ShapeDtypeStruct((window_count, rows, 2 * F), jnp.bfloat16),
        in_specs=[pl.BlockSpec(memory_space=pltpu.SMEM), hbm, hbm] + [vmem] * 6,
        out_specs=vmem,
        scratch_shapes=[
            pltpu.VMEM((rows, length + HOP + LANES), jnp.bfloat16),
            pltpu.VMEM((total, BLOCK), jnp.bfloat16),
            pltpu.VMEM((BLOCK, 2 * F), jnp.bfloat16),
            pltpu.VMEM((total, 2 * F), jnp.float32),
            pltpu.SemaphoreType.DMA((2,)),
        ],
        compiler_params=pltpu.CompilerParams(vmem_limit_bytes=48 * 2**20),
        name="spectra",
    )(
        starts, raw, halo, base_c, base_s,
        turn_c.reshape(blocks, 1, F), turn_s.reshape(blocks, 1, F),
        hann.reshape(blocks, 1, BLOCK), live,
    )


def cross_kernel(split, offsets, low, mid, high, back, out, ext, stack):
    half, span, width = mid.shape
    tiles = width // LANES
    group = out.shape[1]
    chunk = 16
    for w in range(half):
        for j in range(tiles):
            for place, block in enumerate((low, mid, high)):
                piece = block[w, :, j * LANES : (j + 1) * LANES]
                ext[w * tiles + j, place * span : (place + 1) * span, :] = piece.astype(jnp.float32)

    def one_offset(number, carry):
        distance = offsets[number]
        own = span - lax.div(distance, 2)

        def one_chunk(step, carry):
            at_a = pl.ds(own + step * chunk, chunk)
            at_b = pl.ds(own + distance + step * chunk, chunk)
            at = pl.ds(pl.multiple_of(step * chunk, chunk), chunk)
            for j in range(tiles // 2):
                real_sum = jnp.zeros((chunk, LANES), jnp.float32)
                imag_sum = jnp.zeros((chunk, LANES), jnp.float32)
                for w in range(half):
                    a_re = ext[w * tiles + j, at_a, :]
                    a_im = ext[w * tiles + tiles // 2 + j, at_a, :]
                    b_re = ext[w * tiles + j, at_b, :]
                    b_im = ext[w * tiles + tiles // 2 + j, at_b, :]
                    real_sum += a_re * b_re + a_im * b_im
                    imag_sum += a_im * b_re - a_re * b_im
                stack[at, j * LANES : (j + 1) * LANES] = real_sum.astype(jnp.bfloat16)
                lo = width // 2 + j * LANES
                stack[at, lo : lo + LANES] = imag_sum.astype(jnp.bfloat16)
            return carry

        lax.fori_loop(0, span // chunk, one_chunk, 0)
        lagged = jnp.dot(stack[...], back[...], preferred_element_type=jnp.float32)
        owner = lax.div(number, group)
        for part in range(split):
            cols = LAGS // split
            piece = lagged[:, part * cols : (part + 1) * cols]
            out[owner * split + part, lax.rem(number, group)] = piece.astype(jnp.bfloat16)
        return carry

    lax.fori_loop(0, offsets.shape[0], one_offset, 0)


def cross(offsets, low, mid, high, back, split, owners):
    half, span, width = mid.shape
    group = offsets.shape[0] // owners
    vmem = pl.BlockSpec(memory_space=pltpu.VMEM)
    return pl.pallas_call(
        functools.partial(cross_kernel, split),
        out_shape=jax.ShapeDtypeStruct(
            (owners * split, group, span, LAGS // split), jnp.bfloat16
        ),
        in_specs=[pl.BlockSpec(memory_space=pltpu.SMEM)] + [vmem] * 4,
        out_specs=vmem,
        scratch_shapes=[
            pltpu.VMEM((half * width // LANES, 3 * span, LANES), jnp.float32),
            pltpu.VMEM((span, width), jnp.bfloat16),
        ],
        compiler_params=pltpu.CompilerParams(vmem_limit_bytes=48 * 2**20),
        name="cross",
    )(offsets, low, mid, high, back)


def gather_kernel(
    owners, chans, split, scale, offsets, parts, out, landed, total, down, above, mine, theirs,
    send_sems, recv_sems, hop_sems, swap_sems,
):
    peers, group, span, cols = parts.shape
    rows = out.shape[1]
    t = lax.axis_index("tm")
    d = lax.axis_index("chan")
    y = lax.rem(d, split)
    base = d - y
    me = t * split + y
    beneath = lax.rem(d - split + chans, chans)
    upper = lax.rem(d + split, chans)

    def place(p):
        return {"tm": lax.div(p, split), "chan": base + lax.rem(p, split)}

    barrier = pltpu.get_barrier_semaphore()
    for k in range(1, peers):
        pl.semaphore_signal(
            barrier, inc=1, device_id=place(lax.rem(me + k, peers)), device_id_type=MESH
        )
    for c in (beneath, upper):
        pl.semaphore_signal(
            barrier, inc=1, device_id={"tm": t, "chan": c}, device_id_type=MESH
        )
    pl.semaphore_wait(barrier, peers + 1)

    copies = []
    for k in range(1, peers):
        p = lax.rem(me + k, peers)
        copy = pltpu.make_async_remote_copy(
            src_ref=parts.at[p],
            dst_ref=landed.at[k],
            send_sem=send_sems.at[k],
            recv_sem=recv_sems.at[k],
            device_id=place(p),
            device_id_type=MESH,
        )
        copy.start()
        copies.append(copy)
    for copy in copies:
        copy.wait_recv()
    value = parts[me].astype(jnp.float32)
    for k in range(1, peers):
        value += landed[k].astype(jnp.float32)
    total[:, :span, :] = value
    down[...] = value.astype(jnp.bfloat16)
    hop = pltpu.make_async_remote_copy(
        src_ref=down,
        dst_ref=above,
        send_sem=hop_sems.at[0],
        recv_sem=hop_sems.at[1],
        device_id={"tm": t, "chan": beneath},
        device_id_type=MESH,
    )
    hop.start()
    hop.wait_recv()
    inside = (d + split < chans).astype(jnp.float32)
    total[:, span:, :] = above[...].astype(jnp.float32) * inside
    for o in range(group):
        skip = lax.div(offsets[t * group + o], 2)
        mine[o] = total[o, pl.ds(skip + (1 - y) * rows, rows), :] * scale
    swap = pltpu.make_async_remote_copy(
        src_ref=mine,
        dst_ref=theirs,
        send_sem=swap_sems.at[0],
        recv_sem=swap_sems.at[1],
        device_id={"tm": t, "chan": base + 1 - y},
        device_id_type=MESH,
    )
    swap.start()
    swap.wait_recv()
    for o in range(group):
        skip = lax.div(offsets[t * group + o], 2)
        own = total[o, pl.ds(skip + y * rows, rows), :] * scale
        other = theirs[o]
        out[o, :, :cols] = jnp.where(y == 0, own, other)
        out[o, :, cols:] = jnp.where(y == 0, other, own)
    for copy in copies:
        copy.wait_send()
    hop.wait_send()
    swap.wait_send()


def gather(offsets, parts, rows, owners, chans, split, scale):
    peers, group, span, cols = parts.shape
    vmem = pl.BlockSpec(memory_space=pltpu.VMEM)
    return pl.pallas_call(
        functools.partial(gather_kernel, owners, chans, split, scale),
        out_shape=jax.ShapeDtypeStruct((group, rows, LAGS), jnp.float32),
        in_specs=[pl.BlockSpec(memory_space=pltpu.SMEM), vmem],
        out_specs=vmem,
        scratch_shapes=[
            pltpu.VMEM((peers, group, span, cols), jnp.bfloat16),
            pltpu.VMEM((group, 2 * span, cols), jnp.float32),
            pltpu.VMEM((group, span, cols), jnp.bfloat16),
            pltpu.VMEM((group, span, cols), jnp.bfloat16),
            pltpu.VMEM((group, rows, cols), jnp.float32),
            pltpu.VMEM((group, rows, cols), jnp.float32),
            pltpu.SemaphoreType.DMA((peers,)),
            pltpu.SemaphoreType.DMA((peers,)),
            pltpu.SemaphoreType.DMA((2,)),
            pltpu.SemaphoreType.DMA((2,)),
        ],
        compiler_params=pltpu.CompilerParams(
            collective_id=0, has_side_effects=True, vmem_limit_bytes=32 * 2**20
        ),
        name="gather",
    )(offsets, parts)


def local(raw, starts, dead_mask, offsets):
    rows = raw.shape[0]
    window_count = starts.shape[0]
    owners = lax.axis_size("tm")
    chans = lax.axis_size("chan")
    split = MAXOFF // 2 // rows
    half = window_count // split
    halo = shifted(raw[:, :HOP], "tm", -1)
    live = dead_mask.astype(jnp.float32)[:, None]
    white = spectra(raw, halo, starts, live)
    y = lax.rem(lax.axis_index("chan"), split)
    keep = lax.dynamic_slice_in_dim(white, y * half, half, 0)
    give = lax.dynamic_slice_in_dim(white, (1 - y) * half, half, 0)
    got = lax.ppermute(give, "chan", [(i, i ^ 1) for i in range(chans)])
    mid = jnp.where(
        y == 0,
        jnp.concatenate([keep, got], axis=1),
        jnp.concatenate([got, keep], axis=1),
    )
    low = shifted(mid, "chan", split)
    high = shifted(mid, "chan", -split)
    back = inverse_table().astype(jnp.bfloat16)
    parts = cross(offsets, low, mid, high, back, split, owners)
    scale = float((window_count * owners * F) ** -0.5)
    return gather(offsets, parts, rows, owners, chans, split, scale)


def solution(mesh):
    in_specs = (P("chan", "tm"), P("tm"), P("chan"), P())
    out_specs = P("tm", "chan", None)
    return jax.shard_map(local, mesh=mesh, in_specs=in_specs, out_specs=out_specs, check_vma=False)
```

```python
import functools

import jax
import jax.numpy as jnp
from jax import lax
from jax.experimental import pallas as pl
from jax.experimental.pallas import tpu as pltpu
from jax.sharding import PartitionSpec as P

HOP = 4096
F = 640
F0 = 16
LAGS = 256
MAXOFF = 256
LANES = 128
BLOCK = 512
FINE = 64
MESH = pl.DeviceIdType.MESH


def shifted(block, axis, distance):
    devices = range(lax.axis_size(axis))
    route = [(i - distance, i) for i in devices if i - distance in devices]
    return lax.ppermute(block, axis, route)


def waves(samples):
    bins = jnp.arange(F, dtype=jnp.int32) + F0
    phase = samples[:, None] * bins[None, :] % (2 * HOP)
    angle = 2.0 * jnp.pi / (2 * HOP) * phase.astype(jnp.float32)
    return jnp.cos(angle), jnp.sin(angle)


def base_table():
    fine_c, fine_s = waves(jnp.arange(FINE, dtype=jnp.int32))
    wide_c, wide_s = waves(jnp.arange(BLOCK // FINE, dtype=jnp.int32) * FINE)
    fine_c, fine_s = fine_c[None], fine_s[None]
    wide_c, wide_s = wide_c[:, None], wide_s[:, None]
    cosines = wide_c * fine_c - wide_s * fine_s
    sines = wide_s * fine_c + wide_c * fine_s
    return cosines.reshape(BLOCK, F), sines.reshape(BLOCK, F)


def inverse_table():
    bins = jnp.arange(F, dtype=jnp.int32) + F0
    lagged = jnp.arange(LAGS, dtype=jnp.int32) - LAGS // 2
    phase = jnp.mod(bins[:, None] * lagged[None, :], 2 * HOP)
    angle = 2.0 * jnp.pi / (2 * HOP) * phase.astype(jnp.float32)
    return jnp.concatenate([jnp.cos(angle), -jnp.sin(angle)], axis=0)


def spectra_kernel(
    starts, raw, halo, base_c, base_s, turn_c, turn_s, hann, live, white, pad, tap, table,
    later_tap, later_table, acc, sems
):
    rows, length = raw.shape
    window_count = starts.shape[0]
    first = pltpu.make_async_copy(raw, pad.at[:, pl.ds(0, length)], sems.at[0])
    second = pltpu.make_async_copy(halo, pad.at[:, pl.ds(length, HOP)], sems.at[1])
    first.start()
    second.start()
    acc[...] = jnp.zeros_like(acc)
    lane = lax.broadcasted_iota(jnp.int32, (rows, LANES), 1)
    first.wait()
    second.wait()

    def prepare(number, tap, table):
        ct, st = turn_c[number], turn_s[number]
        bc, bs = base_c[...], base_s[...]
        table[:, :F] = (bc * ct - bs * st).astype(jnp.bfloat16)
        table[:, F:] = (-(bs * ct + bc * st)).astype(jnp.bfloat16)
        taper = hann[number]
        for w in range(window_count):
            begin = starts[w]
            rest = lax.rem(begin, LANES)
            column = pl.multiple_of(begin - rest + number * BLOCK, LANES)
            turn = lax.rem(LANES - rest, LANES)
            keep = lane < LANES - rest
            rolled = None
            for j in range(BLOCK // LANES + 1):
                piece = pad[:, pl.ds(pl.multiple_of(column + j * LANES, LANES), LANES)]
                following = pltpu.roll(piece.astype(jnp.float32), turn, 1)
                if j:
                    lo = (j - 1) * LANES
                    value = jnp.where(keep, rolled, following) * taper[:, lo : lo + LANES]
                    tap[w * rows : (w + 1) * rows, lo : lo + LANES] = value.astype(jnp.bfloat16)
                rolled = following

    blocks = 2 * HOP // BLOCK
    prepare(0, tap, table)

    def step(number, carry):
        prepare(2 * number + 1, later_tap, later_table)
        acc[...] += jnp.dot(tap[...], table[...], preferred_element_type=jnp.float32)
        prepare(lax.rem(2 * number + 2, blocks), tap, table)
        acc[...] += jnp.dot(later_tap[...], later_table[...], preferred_element_type=jnp.float32)
        return carry

    lax.fori_loop(0, blocks // 2, step, 0)

    def whiten(w, carry):
        at = pl.ds(pl.multiple_of(w * rows, rows), rows)
        real_part = acc[at, :F]
        imag_part = acc[at, F:]
        amplitude = jnp.sqrt(real_part * real_part + imag_part * imag_part)
        level = jnp.mean(amplitude, axis=-1, keepdims=True)
        scaled = live[...] / (amplitude + 0.1 * level + 1e-06)
        white[w, :, :F] = (real_part * scaled).astype(jnp.bfloat16)
        white[w, :, F:] = (imag_part * scaled).astype(jnp.bfloat16)
        return carry

    lax.fori_loop(0, window_count, whiten, 0)


def spectra(raw, halo, starts, live):
    rows, length = raw.shape
    window_count = starts.shape[0]
    blocks = 2 * HOP // BLOCK
    base_c, base_s = base_table()
    turn_c, turn_s = waves(jnp.arange(blocks, dtype=jnp.int32) * BLOCK)
    sample = jnp.arange(2 * HOP, dtype=jnp.float32)
    hann = 0.5 - 0.5 * jnp.cos(2.0 * jnp.pi * sample / (2 * HOP))
    vmem = pl.BlockSpec(memory_space=pltpu.VMEM)
    hbm = pl.BlockSpec(memory_space=pl.ANY)
    total = window_count * rows
    return pl.pallas_call(
        spectra_kernel,
        out_shape=jax.ShapeDtypeStruct((window_count, rows, 2 * F), jnp.bfloat16),
        in_specs=[pl.BlockSpec(memory_space=pltpu.SMEM), hbm, hbm] + [vmem] * 6,
        out_specs=vmem,
        scratch_shapes=[
            pltpu.VMEM((rows, length + HOP + LANES), jnp.bfloat16),
            pltpu.VMEM((total, BLOCK), jnp.bfloat16),
            pltpu.VMEM((BLOCK, 2 * F), jnp.bfloat16),
            pltpu.VMEM((total, BLOCK), jnp.bfloat16),
            pltpu.VMEM((BLOCK, 2 * F), jnp.bfloat16),
            pltpu.VMEM((total, 2 * F), jnp.float32),
            pltpu.SemaphoreType.DMA((2,)),
        ],
        compiler_params=pltpu.CompilerParams(vmem_limit_bytes=48 * 2**20),
        name="spectra",
    )(
        starts, raw, halo, base_c, base_s,
        turn_c.reshape(blocks, 1, F), turn_s.reshape(blocks, 1, F),
        hann.reshape(blocks, 1, BLOCK), live,
    )


def cross_kernel(split, offsets, *refs):
    *blocks, back, out, ext, stack = refs
    half, rows, width = blocks[0].shape
    span = split * rows
    tiles = width // LANES
    group = out.shape[1]
    chunk = 16
    y = lax.rem(lax.axis_index("chan"), split)
    for number, block in enumerate(blocks):
        position = y if number % 2 == 0 else 1 - y
        at = pl.ds(pl.multiple_of(number // 2 * span + position * rows, rows), rows)
        for w in range(half):
            for j in range(tiles):
                piece = block[w, :, j * LANES : (j + 1) * LANES]
                ext[w * tiles + j, at, :] = piece.astype(jnp.float32)

    def one_offset(number, carry):
        distance = offsets[number]
        own = span - lax.div(distance, 2)

        def one_chunk(step, carry):
            at_a = pl.ds(own + step * chunk, chunk)
            at_b = pl.ds(own + distance + step * chunk, chunk)
            at = pl.ds(pl.multiple_of(step * chunk, chunk), chunk)
            for j in range(tiles // 2):
                real_sum = jnp.zeros((chunk, LANES), jnp.float32)
                imag_sum = jnp.zeros((chunk, LANES), jnp.float32)
                for w in range(half):
                    a_re = ext[w * tiles + j, at_a, :]
                    a_im = ext[w * tiles + tiles // 2 + j, at_a, :]
                    b_re = ext[w * tiles + j, at_b, :]
                    b_im = ext[w * tiles + tiles // 2 + j, at_b, :]
                    real_sum += a_re * b_re + a_im * b_im
                    imag_sum += a_im * b_re - a_re * b_im
                stack[at, j * LANES : (j + 1) * LANES] = real_sum.astype(jnp.bfloat16)
                lo = width // 2 + j * LANES
                stack[at, lo : lo + LANES] = imag_sum.astype(jnp.bfloat16)
            return carry

        lax.fori_loop(0, span // chunk, one_chunk, 0)
        lagged = jnp.dot(stack[...], back[...], preferred_element_type=jnp.float32)
        owner = lax.div(number, group)
        for part in range(split):
            cols = LAGS // split
            piece = lagged[:, part * cols : (part + 1) * cols]
            out[owner * split + part, lax.rem(number, group)] = piece.astype(jnp.bfloat16)
        return carry

    lax.fori_loop(0, offsets.shape[0], one_offset, 0)


def cross(offsets, blocks, back, split, owners):
    half, rows, width = blocks[0].shape
    span = split * rows
    group = offsets.shape[0] // owners
    vmem = pl.BlockSpec(memory_space=pltpu.VMEM)
    return pl.pallas_call(
        functools.partial(cross_kernel, split),
        out_shape=jax.ShapeDtypeStruct(
            (owners * split, group, span, LAGS // split), jnp.bfloat16
        ),
        in_specs=[pl.BlockSpec(memory_space=pltpu.SMEM)] + [vmem] * (len(blocks) + 1),
        out_specs=vmem,
        scratch_shapes=[
            pltpu.VMEM((half * width // LANES, 3 * span, LANES), jnp.float32),
            pltpu.VMEM((span, width), jnp.bfloat16),
        ],
        compiler_params=pltpu.CompilerParams(vmem_limit_bytes=48 * 2**20),
        name="cross",
    )(offsets, *blocks, back)


def gather_kernel(
    owners, chans, split, scale, offsets, parts, out, landed, total, down, above, mine, theirs,
    send_sems, recv_sems, hop_sems, swap_sems,
):
    peers, group, span, cols = parts.shape
    rows = out.shape[1]
    t = lax.axis_index("tm")
    d = lax.axis_index("chan")
    y = lax.rem(d, split)
    base = d - y
    me = t * split + y
    beneath = lax.rem(d - split + chans, chans)
    upper = lax.rem(d + split, chans)

    def place(p):
        return {"tm": lax.div(p, split), "chan": base + lax.rem(p, split)}

    barrier = pltpu.get_barrier_semaphore()
    for k in range(1, peers):
        pl.semaphore_signal(
            barrier, inc=1, device_id=place(lax.rem(me + k, peers)), device_id_type=MESH
        )
    for c in (beneath, upper):
        pl.semaphore_signal(
            barrier, inc=1, device_id={"tm": t, "chan": c}, device_id_type=MESH
        )
    pl.semaphore_wait(barrier, peers + 1)

    copies = []
    for k in range(1, peers):
        p = lax.rem(me + k, peers)
        copy = pltpu.make_async_remote_copy(
            src_ref=parts.at[p],
            dst_ref=landed.at[k],
            send_sem=send_sems.at[k],
            recv_sem=recv_sems.at[k],
            device_id=place(p),
            device_id_type=MESH,
        )
        copy.start()
        copies.append(copy)
    for copy in copies:
        copy.wait_recv()
    value = parts[me].astype(jnp.float32)
    for k in range(1, peers):
        value += landed[k].astype(jnp.float32)
    total[:, :span, :] = value
    down[...] = value.astype(jnp.bfloat16)
    hop = pltpu.make_async_remote_copy(
        src_ref=down,
        dst_ref=above,
        send_sem=hop_sems.at[0],
        recv_sem=hop_sems.at[1],
        device_id={"tm": t, "chan": beneath},
        device_id_type=MESH,
    )
    hop.start()
    hop.wait_recv()
    inside = (d + split < chans).astype(jnp.float32)
    total[:, span:, :] = above[...].astype(jnp.float32) * inside
    for o in range(group):
        skip = lax.div(offsets[t * group + o], 2)
        mine[o] = total[o, pl.ds(skip + (1 - y) * rows, rows), :] * scale
    swap = pltpu.make_async_remote_copy(
        src_ref=mine,
        dst_ref=theirs,
        send_sem=swap_sems.at[0],
        recv_sem=swap_sems.at[1],
        device_id={"tm": t, "chan": base + 1 - y},
        device_id_type=MESH,
    )
    swap.start()
    swap.wait_recv()
    for o in range(group):
        skip = lax.div(offsets[t * group + o], 2)
        own = total[o, pl.ds(skip + y * rows, rows), :] * scale
        other = theirs[o]
        out[o, :, :cols] = jnp.where(y == 0, own, other)
        out[o, :, cols:] = jnp.where(y == 0, other, own)
    for copy in copies:
        copy.wait_send()
    hop.wait_send()
    swap.wait_send()


def gather(offsets, parts, rows, owners, chans, split, scale):
    peers, group, span, cols = parts.shape
    vmem = pl.BlockSpec(memory_space=pltpu.VMEM)
    return pl.pallas_call(
        functools.partial(gather_kernel, owners, chans, split, scale),
        out_shape=jax.ShapeDtypeStruct((group, rows, LAGS), jnp.float32),
        in_specs=[pl.BlockSpec(memory_space=pltpu.SMEM), vmem],
        out_specs=vmem,
        scratch_shapes=[
            pltpu.VMEM((peers, group, span, cols), jnp.bfloat16),
            pltpu.VMEM((group, 2 * span, cols), jnp.float32),
            pltpu.VMEM((group, span, cols), jnp.bfloat16),
            pltpu.VMEM((group, span, cols), jnp.bfloat16),
            pltpu.VMEM((group, rows, cols), jnp.float32),
            pltpu.VMEM((group, rows, cols), jnp.float32),
            pltpu.SemaphoreType.DMA((peers,)),
            pltpu.SemaphoreType.DMA((peers,)),
            pltpu.SemaphoreType.DMA((2,)),
            pltpu.SemaphoreType.DMA((2,)),
        ],
        compiler_params=pltpu.CompilerParams(
            collective_id=0, has_side_effects=True, vmem_limit_bytes=32 * 2**20
        ),
        name="gather",
    )(offsets, parts)


def local(raw, starts, dead_mask, offsets):
    rows = raw.shape[0]
    window_count = starts.shape[0]
    owners = lax.axis_size("tm")
    chans = lax.axis_size("chan")
    split = MAXOFF // 2 // rows
    half = window_count // split
    halo = shifted(raw[:, :HOP], "tm", -1)
    live = dead_mask.astype(jnp.float32)[:, None]
    white = spectra(raw, halo, starts, live)
    y = lax.rem(lax.axis_index("chan"), split)
    keep = lax.dynamic_slice_in_dim(white, y * half, half, 0)
    give = lax.dynamic_slice_in_dim(white, (1 - y) * half, half, 0)
    got = lax.ppermute(give, "chan", [(i, i ^ 1) for i in range(chans)])
    blocks = [
        shifted(keep, "chan", split), shifted(got, "chan", split),
        keep, got,
        shifted(keep, "chan", -split), shifted(got, "chan", -split),
    ]
    back = inverse_table().astype(jnp.bfloat16)
    parts = cross(offsets, blocks, back, split, owners)
    scale = float((window_count * owners * F) ** -0.5)
    return gather(offsets, parts, rows, owners, chans, split, scale)


def solution(mesh):
    in_specs = (P("chan", "tm"), P("tm"), P("chan"), P())
    out_specs = P("tm", "chan", None)
    return jax.shard_map(local, mesh=mesh, in_specs=in_specs, out_specs=out_specs, check_vma=False)
```

```python
import functools

import jax
import jax.numpy as jnp
from jax import lax
from jax.experimental import pallas as pl
from jax.experimental.pallas import tpu as pltpu
from jax.sharding import PartitionSpec as P

HOP = 4096
F = 640
F0 = 16
LAGS = 256
MAXOFF = 256
LANES = 128
BLOCK = 512
FINE = 64
MESH = pl.DeviceIdType.MESH


def shifted(block, axis, distance):
    devices = range(lax.axis_size(axis))
    route = [(i - distance, i) for i in devices if i - distance in devices]
    return lax.ppermute(block, axis, route)


def waves(samples):
    bins = jnp.arange(F, dtype=jnp.int32) + F0
    phase = samples[:, None] * bins[None, :] % (2 * HOP)
    angle = 2.0 * jnp.pi / (2 * HOP) * phase.astype(jnp.float32)
    return jnp.cos(angle), jnp.sin(angle)


def base_table():
    fine_c, fine_s = waves(jnp.arange(FINE, dtype=jnp.int32))
    wide_c, wide_s = waves(jnp.arange(BLOCK // FINE, dtype=jnp.int32) * FINE)
    fine_c, fine_s = fine_c[None], fine_s[None]
    wide_c, wide_s = wide_c[:, None], wide_s[:, None]
    cosines = wide_c * fine_c - wide_s * fine_s
    sines = wide_s * fine_c + wide_c * fine_s
    return cosines.reshape(BLOCK, F), sines.reshape(BLOCK, F)


def inverse_table():
    bins = jnp.arange(F, dtype=jnp.int32) + F0
    lagged = jnp.arange(LAGS, dtype=jnp.int32) - LAGS // 2
    phase = jnp.mod(bins[:, None] * lagged[None, :], 2 * HOP)
    angle = 2.0 * jnp.pi / (2 * HOP) * phase.astype(jnp.float32)
    return jnp.concatenate([jnp.cos(angle), -jnp.sin(angle)], axis=0)


def spectra_kernel(
    starts, raw, halo, base_c, base_s, turn_c, turn_s, hann, live, white, pad, tap, table,
    later_tap, later_table, acc, sems
):
    rows, length = raw.shape
    window_count = starts.shape[0]
    first = pltpu.make_async_copy(raw, pad.at[:, pl.ds(0, length)], sems.at[0])
    second = pltpu.make_async_copy(halo, pad.at[:, pl.ds(length, HOP)], sems.at[1])
    first.start()
    second.start()
    acc[...] = jnp.zeros_like(acc)
    lane = lax.broadcasted_iota(jnp.int32, (rows, LANES), 1)
    first.wait()
    second.wait()

    def prepare(number, tap, table):
        ct, st = turn_c[number], turn_s[number]
        bc, bs = base_c[...], base_s[...]
        table[:, :F] = (bc * ct - bs * st).astype(jnp.bfloat16)
        table[:, F:] = (-(bs * ct + bc * st)).astype(jnp.bfloat16)
        taper = hann[number]
        for w in range(window_count):
            begin = starts[w]
            rest = lax.rem(begin, LANES)
            column = pl.multiple_of(begin - rest + number * BLOCK, LANES)
            turn = lax.rem(LANES - rest, LANES)
            keep = lane < LANES - rest
            rolled = None
            for j in range(BLOCK // LANES + 1):
                piece = pad[:, pl.ds(pl.multiple_of(column + j * LANES, LANES), LANES)]
                following = pltpu.roll(piece.astype(jnp.float32), turn, 1)
                if j:
                    lo = (j - 1) * LANES
                    value = jnp.where(keep, rolled, following) * taper[:, lo : lo + LANES]
                    tap[w * rows : (w + 1) * rows, lo : lo + LANES] = value.astype(jnp.bfloat16)
                rolled = following

    blocks = 2 * HOP // BLOCK
    prepare(0, tap, table)

    def step(number, carry):
        prepare(2 * number + 1, later_tap, later_table)
        acc[...] += jnp.dot(tap[...], table[...], preferred_element_type=jnp.float32)
        prepare(lax.rem(2 * number + 2, blocks), tap, table)
        acc[...] += jnp.dot(later_tap[...], later_table[...], preferred_element_type=jnp.float32)
        return carry

    lax.fori_loop(0, blocks // 2, step, 0)

    def whiten(w, carry):
        at = pl.ds(pl.multiple_of(w * rows, rows), rows)
        real_part = acc[at, :F]
        imag_part = acc[at, F:]
        amplitude = jnp.sqrt(real_part * real_part + imag_part * imag_part)
        level = jnp.mean(amplitude, axis=-1, keepdims=True)
        scaled = live[...] / (amplitude + 0.1 * level + 1e-06)
        white[w, :, :F] = (real_part * scaled).astype(jnp.bfloat16)
        white[w, :, F:] = (imag_part * scaled).astype(jnp.bfloat16)
        return carry

    lax.fori_loop(0, window_count, whiten, 0)


def spectra(raw, halo, starts, live):
    rows, length = raw.shape
    window_count = starts.shape[0]
    blocks = 2 * HOP // BLOCK
    base_c, base_s = base_table()
    turn_c, turn_s = waves(jnp.arange(blocks, dtype=jnp.int32) * BLOCK)
    sample = jnp.arange(2 * HOP, dtype=jnp.float32)
    hann = 0.5 - 0.5 * jnp.cos(2.0 * jnp.pi * sample / (2 * HOP))
    vmem = pl.BlockSpec(memory_space=pltpu.VMEM)
    hbm = pl.BlockSpec(memory_space=pl.ANY)
    total = window_count * rows
    return pl.pallas_call(
        spectra_kernel,
        out_shape=jax.ShapeDtypeStruct((window_count, rows, 2 * F), jnp.bfloat16),
        in_specs=[pl.BlockSpec(memory_space=pltpu.SMEM), hbm, hbm] + [vmem] * 6,
        out_specs=vmem,
        scratch_shapes=[
            pltpu.VMEM((rows, length + HOP + LANES), jnp.bfloat16),
            pltpu.VMEM((total, BLOCK), jnp.bfloat16),
            pltpu.VMEM((BLOCK, 2 * F), jnp.bfloat16),
            pltpu.VMEM((total, BLOCK), jnp.bfloat16),
            pltpu.VMEM((BLOCK, 2 * F), jnp.bfloat16),
            pltpu.VMEM((total, 2 * F), jnp.float32),
            pltpu.SemaphoreType.DMA((2,)),
        ],
        compiler_params=pltpu.CompilerParams(vmem_limit_bytes=48 * 2**20),
        name="spectra",
    )(
        starts, raw, halo, base_c, base_s,
        turn_c.reshape(blocks, 1, F), turn_s.reshape(blocks, 1, F),
        hann.reshape(blocks, 1, BLOCK), live,
    )


def cross_kernel(owners, chans, split, scale, offsets, *refs):
    (*blocks, back, out, ext, stack, parts, landed, total, down, above, mine, theirs,
     send_sems, recv_sems, hop_sems, swap_sems) = refs
    half, rows, width = blocks[0].shape
    span = split * rows
    tiles = width // LANES
    peers, group, _, cols = parts.shape
    chunk = 16
    t = lax.axis_index("tm")
    d = lax.axis_index("chan")
    y = lax.rem(d, split)
    base = d - y
    me = t * split + y
    beneath = lax.rem(d - split + chans, chans)
    upper = lax.rem(d + split, chans)

    def place(p):
        return {"tm": lax.div(p, split), "chan": base + lax.rem(p, split)}

    barrier = pltpu.get_barrier_semaphore()
    for k in range(1, peers):
        pl.semaphore_signal(
            barrier, inc=1, device_id=place(lax.rem(me + k, peers)), device_id_type=MESH
        )
    for c in (beneath, upper):
        pl.semaphore_signal(
            barrier, inc=1, device_id={"tm": t, "chan": c}, device_id_type=MESH
        )

    for number, block in enumerate(blocks):
        position = y if number % 2 == 0 else 1 - y
        at = pl.ds(pl.multiple_of(number // 2 * span + position * rows, rows), rows)
        for w in range(half):
            for j in range(tiles):
                piece = block[w, :, j * LANES : (j + 1) * LANES]
                ext[w * tiles + j, at, :] = piece.astype(jnp.float32)

    def one_offset(owner, place_in):
        distance = offsets[owner * group + place_in]
        own = span - lax.div(distance, 2)

        def one_chunk(step, carry):
            at_a = pl.ds(own + step * chunk, chunk)
            at_b = pl.ds(own + distance + step * chunk, chunk)
            at = pl.ds(pl.multiple_of(step * chunk, chunk), chunk)
            for j in range(tiles // 2):
                real_sum = jnp.zeros((chunk, LANES), jnp.float32)
                imag_sum = jnp.zeros((chunk, LANES), jnp.float32)
                for w in range(half):
                    a_re = ext[w * tiles + j, at_a, :]
                    a_im = ext[w * tiles + tiles // 2 + j, at_a, :]
                    b_re = ext[w * tiles + j, at_b, :]
                    b_im = ext[w * tiles + tiles // 2 + j, at_b, :]
                    real_sum += a_re * b_re + a_im * b_im
                    imag_sum += a_im * b_re - a_re * b_im
                stack[at, j * LANES : (j + 1) * LANES] = real_sum.astype(jnp.bfloat16)
                lo = width // 2 + j * LANES
                stack[at, lo : lo + LANES] = imag_sum.astype(jnp.bfloat16)
            return carry

        lax.fori_loop(0, span // chunk, one_chunk, 0)
        lagged = jnp.dot(stack[...], back[...], preferred_element_type=jnp.float32)
        for part in range(split):
            piece = lagged[:, part * cols : (part + 1) * cols]
            parts[owner * split + part, place_in] = piece.astype(jnp.bfloat16)

    copies = []
    for s in range(owners):
        owner = lax.rem(t + 1 + s, owners)

        def body(place_in, carry, owner=owner):
            one_offset(owner, place_in)
            return carry

        lax.fori_loop(0, group, body, 0)
        if s == 0:
            pl.semaphore_wait(barrier, peers + 1)
        for part in range(split) if s < owners - 1 else (1 - y,):
            p = owner * split + part
            k = lax.rem(p - me + peers, peers)
            copy = pltpu.make_async_remote_copy(
                src_ref=parts.at[p],
                dst_ref=landed.at[k],
                send_sem=send_sems.at[k],
                recv_sem=recv_sems.at[k],
                device_id=place(p),
                device_id_type=MESH,
            )
            copy.start()
            copies.append(copy)
    for copy in copies:
        copy.wait_recv()
    value = parts[me].astype(jnp.float32)
    for k in range(1, peers):
        value += landed[k].astype(jnp.float32)
    total[:, :span, :] = value
    down[...] = value.astype(jnp.bfloat16)
    hop = pltpu.make_async_remote_copy(
        src_ref=down,
        dst_ref=above,
        send_sem=hop_sems.at[0],
        recv_sem=hop_sems.at[1],
        device_id={"tm": t, "chan": beneath},
        device_id_type=MESH,
    )
    hop.start()
    hop.wait_recv()
    inside = (d + split < chans).astype(jnp.float32)
    total[:, span:, :] = above[...].astype(jnp.float32) * inside
    for o in range(group):
        skip = lax.div(offsets[t * group + o], 2)
        mine[o] = total[o, pl.ds(skip + (1 - y) * rows, rows), :] * scale
    swap = pltpu.make_async_remote_copy(
        src_ref=mine,
        dst_ref=theirs,
        send_sem=swap_sems.at[0],
        recv_sem=swap_sems.at[1],
        device_id={"tm": t, "chan": base + 1 - y},
        device_id_type=MESH,
    )
    swap.start()
    swap.wait_recv()
    for o in range(group):
        skip = lax.div(offsets[t * group + o], 2)
        own = total[o, pl.ds(skip + y * rows, rows), :] * scale
        other = theirs[o]
        out[o, :, :cols] = jnp.where(y == 0, own, other)
        out[o, :, cols:] = jnp.where(y == 0, other, own)
    for copy in copies:
        copy.wait_send()
    hop.wait_send()
    swap.wait_send()


def cross(offsets, blocks, back, owners, chans, split, scale):
    half, rows, width = blocks[0].shape
    span = split * rows
    group = offsets.shape[0] // owners
    peers = owners * split
    cols = LAGS // split
    vmem = pl.BlockSpec(memory_space=pltpu.VMEM)
    return pl.pallas_call(
        functools.partial(cross_kernel, owners, chans, split, scale),
        out_shape=jax.ShapeDtypeStruct((group, rows, LAGS), jnp.float32),
        in_specs=[pl.BlockSpec(memory_space=pltpu.SMEM)] + [vmem] * (len(blocks) + 1),
        out_specs=vmem,
        scratch_shapes=[
            pltpu.VMEM((half * width // LANES, 3 * span, LANES), jnp.float32),
            pltpu.VMEM((span, width), jnp.bfloat16),
            pltpu.VMEM((peers, group, span, cols), jnp.bfloat16),
            pltpu.VMEM((peers, group, span, cols), jnp.bfloat16),
            pltpu.VMEM((group, 2 * span, cols), jnp.float32),
            pltpu.VMEM((group, span, cols), jnp.bfloat16),
            pltpu.VMEM((group, span, cols), jnp.bfloat16),
            pltpu.VMEM((group, rows, cols), jnp.float32),
            pltpu.VMEM((group, rows, cols), jnp.float32),
            pltpu.SemaphoreType.DMA((peers,)),
            pltpu.SemaphoreType.DMA((peers,)),
            pltpu.SemaphoreType.DMA((2,)),
            pltpu.SemaphoreType.DMA((2,)),
        ],
        compiler_params=pltpu.CompilerParams(
            collective_id=0, has_side_effects=True, vmem_limit_bytes=40 * 2**20
        ),
        name="cross",
    )(offsets, *blocks, back)


def local(raw, starts, dead_mask, offsets):
    rows = raw.shape[0]
    window_count = starts.shape[0]
    owners = lax.axis_size("tm")
    chans = lax.axis_size("chan")
    split = MAXOFF // 2 // rows
    half = window_count // split
    halo = shifted(raw[:, :HOP], "tm", -1)
    live = dead_mask.astype(jnp.float32)[:, None]
    white = spectra(raw, halo, starts, live)
    y = lax.rem(lax.axis_index("chan"), split)
    keep = lax.dynamic_slice_in_dim(white, y * half, half, 0)
    give = lax.dynamic_slice_in_dim(white, (1 - y) * half, half, 0)
    got = lax.ppermute(give, "chan", [(i, i ^ 1) for i in range(chans)])
    blocks = [
        shifted(keep, "chan", split), shifted(got, "chan", split),
        keep, got,
        shifted(keep, "chan", -split), shifted(got, "chan", -split),
    ]
    back = inverse_table().astype(jnp.bfloat16)
    scale = float((window_count * owners * F) ** -0.5)
    return cross(offsets, blocks, back, owners, chans, split, scale)


def solution(mesh):
    in_specs = (P("chan", "tm"), P("tm"), P("chan"), P())
    out_specs = P("tm", "chan", None)
    return jax.shard_map(local, mesh=mesh, in_specs=in_specs, out_specs=out_specs, check_vma=False)
```

```python
import functools

import jax
import jax.numpy as jnp
from jax import lax
from jax.experimental import pallas as pl
from jax.experimental.pallas import tpu as pltpu
from jax.sharding import PartitionSpec as P

HOP = 4096
F = 640
F0 = 16
LAGS = 256
MAXOFF = 256
LANES = 128
BLOCK = 512
FINE = 64
MESH = pl.DeviceIdType.MESH


def shifted(block, axis, distance):
    devices = range(lax.axis_size(axis))
    route = [(i - distance, i) for i in devices if i - distance in devices]
    return lax.ppermute(block, axis, route)


def waves(samples):
    bins = jnp.arange(F, dtype=jnp.int32) + F0
    phase = samples[:, None] * bins[None, :] % (2 * HOP)
    angle = 2.0 * jnp.pi / (2 * HOP) * phase.astype(jnp.float32)
    return jnp.cos(angle), jnp.sin(angle)


def base_table():
    fine_c, fine_s = waves(jnp.arange(FINE, dtype=jnp.int32))
    wide_c, wide_s = waves(jnp.arange(BLOCK // FINE, dtype=jnp.int32) * FINE)
    fine_c, fine_s = fine_c[None], fine_s[None]
    wide_c, wide_s = wide_c[:, None], wide_s[:, None]
    cosines = wide_c * fine_c - wide_s * fine_s
    sines = wide_s * fine_c + wide_c * fine_s
    return cosines.reshape(BLOCK, F), sines.reshape(BLOCK, F)


def inverse_table():
    bins = jnp.arange(F, dtype=jnp.int32) + F0
    lagged = jnp.arange(LAGS, dtype=jnp.int32) - LAGS // 2
    phase = jnp.mod(bins[:, None] * lagged[None, :], 2 * HOP)
    angle = 2.0 * jnp.pi / (2 * HOP) * phase.astype(jnp.float32)
    return jnp.concatenate([jnp.cos(angle), -jnp.sin(angle)], axis=0)


def spectra_kernel(
    starts, raw, halo, base_c, base_s, turn_c, turn_s, hann, live, white, pad, tap, table,
    later_tap, later_table, acc, sems
):
    rows, length = raw.shape
    window_count = starts.shape[0]
    first = pltpu.make_async_copy(raw, pad.at[:, pl.ds(0, length)], sems.at[0])
    second = pltpu.make_async_copy(halo, pad.at[:, pl.ds(length, HOP)], sems.at[1])
    first.start()
    second.start()
    acc[...] = jnp.zeros_like(acc)
    lane = lax.broadcasted_iota(jnp.int32, (rows, LANES), 1)
    first.wait()
    second.wait()

    def prepare(number, tap, table):
        ct, st = turn_c[number], turn_s[number]
        bc, bs = base_c[...], base_s[...]
        table[:, :F] = (bc * ct - bs * st).astype(jnp.bfloat16)
        table[:, F:] = (-(bs * ct + bc * st)).astype(jnp.bfloat16)
        taper = hann[number]
        for w in range(window_count):
            begin = starts[w]
            rest = lax.rem(begin, LANES)
            column = pl.multiple_of(begin - rest + number * BLOCK, LANES)
            turn = lax.rem(LANES - rest, LANES)
            keep = lane < LANES - rest
            rolled = None
            for j in range(BLOCK // LANES + 1):
                piece = pad[:, pl.ds(pl.multiple_of(column + j * LANES, LANES), LANES)]
                following = pltpu.roll(piece.astype(jnp.float32), turn, 1)
                if j:
                    lo = (j - 1) * LANES
                    value = jnp.where(keep, rolled, following) * taper[:, lo : lo + LANES]
                    tap[w * rows : (w + 1) * rows, lo : lo + LANES] = value.astype(jnp.bfloat16)
                rolled = following

    blocks = 2 * HOP // BLOCK
    prepare(0, tap, table)

    def step(number, carry):
        prepare(2 * number + 1, later_tap, later_table)
        acc[...] += jnp.dot(tap[...], table[...], preferred_element_type=jnp.float32)
        prepare(lax.rem(2 * number + 2, blocks), tap, table)
        acc[...] += jnp.dot(later_tap[...], later_table[...], preferred_element_type=jnp.float32)
        return carry

    lax.fori_loop(0, blocks // 2, step, 0)

    def whiten(w, carry):
        at = pl.ds(pl.multiple_of(w * rows, rows), rows)
        real_part = acc[at, :F]
        imag_part = acc[at, F:]
        amplitude = jnp.sqrt(real_part * real_part + imag_part * imag_part)
        level = jnp.mean(amplitude, axis=-1, keepdims=True)
        scaled = live[...] / (amplitude + 0.1 * level + 1e-06)
        white[w, :, :F] = (real_part * scaled).astype(jnp.bfloat16)
        white[w, :, F:] = (imag_part * scaled).astype(jnp.bfloat16)
        return carry

    lax.fori_loop(0, window_count, whiten, 0)


def spectra(raw, halo, starts, live):
    rows, length = raw.shape
    window_count = starts.shape[0]
    blocks = 2 * HOP // BLOCK
    base_c, base_s = base_table()
    turn_c, turn_s = waves(jnp.arange(blocks, dtype=jnp.int32) * BLOCK)
    sample = jnp.arange(2 * HOP, dtype=jnp.float32)
    hann = 0.5 - 0.5 * jnp.cos(2.0 * jnp.pi * sample / (2 * HOP))
    vmem = pl.BlockSpec(memory_space=pltpu.VMEM)
    hbm = pl.BlockSpec(memory_space=pl.ANY)
    total = window_count * rows
    return pl.pallas_call(
        spectra_kernel,
        out_shape=jax.ShapeDtypeStruct((window_count, rows, 2 * F), jnp.bfloat16),
        in_specs=[pl.BlockSpec(memory_space=pltpu.SMEM), hbm, hbm] + [vmem] * 6,
        out_specs=vmem,
        scratch_shapes=[
            pltpu.VMEM((rows, length + HOP + LANES), jnp.bfloat16),
            pltpu.VMEM((total, BLOCK), jnp.bfloat16),
            pltpu.VMEM((BLOCK, 2 * F), jnp.bfloat16),
            pltpu.VMEM((total, BLOCK), jnp.bfloat16),
            pltpu.VMEM((BLOCK, 2 * F), jnp.bfloat16),
            pltpu.VMEM((total, 2 * F), jnp.float32),
            pltpu.SemaphoreType.DMA((2,)),
        ],
        compiler_params=pltpu.CompilerParams(vmem_limit_bytes=48 * 2**20),
        name="spectra",
    )(
        starts, raw, halo, base_c, base_s,
        turn_c.reshape(blocks, 1, F), turn_s.reshape(blocks, 1, F),
        hann.reshape(blocks, 1, BLOCK), live,
    )


def cross_kernel(owners, chans, split, scale, offsets, *refs):
    (keep, give, back, out, ext, stack, parts, landed, total, down, above, mine, theirs,
     send_sems, recv_sems, hop_sems, swap_sems, bufs, out_sems, in_sems) = refs
    half, rows, width = keep.shape
    span = split * rows
    tiles = width // LANES
    peers, group, _, cols = parts.shape
    chunk = 16
    t = lax.axis_index("tm")
    d = lax.axis_index("chan")
    y = lax.rem(d, split)
    base = d - y
    me = t * split + y
    beneath = lax.rem(d - split + chans, chans)
    upper = lax.rem(d + split, chans)

    def place(p):
        return {"tm": lax.div(p, split), "chan": base + lax.rem(p, split)}

    barrier = pltpu.get_barrier_semaphore()
    for k in range(1, peers):
        pl.semaphore_signal(
            barrier, inc=1, device_id=place(lax.rem(me + k, peers)), device_id_type=MESH
        )
    for c in (beneath, upper):
        pl.semaphore_signal(
            barrier, inc=1, device_id={"tm": t, "chan": c}, device_id_type=MESH
        )

    pl.semaphore_wait(barrier, peers + 1)

    def remote(src, dst, number, chan):
        return pltpu.make_async_remote_copy(
            src_ref=src,
            dst_ref=dst,
            send_sem=out_sems.at[number],
            recv_sem=in_sems.at[number],
            device_id={"tm": t, "chan": chan},
            device_id_type=MESH,
        )

    partner = base + 1 - y
    pair = [remote(give.at[w], bufs.at[0, w], w, partner) for w in range(half)]
    lower = [remote(keep, bufs.at[3], half, beneath)]
    raised = [remote(keep, bufs.at[1], half + 1, upper)]
    for w in range(half):
        lower.append(remote(bufs.at[0, w], bufs.at[4, w], half + 2 + w, beneath))
        raised.append(remote(bufs.at[0, w], bufs.at[2, w], 2 * half + 2 + w, upper))
    has_below = d >= split
    has_above = d + split < chans

    for copy in pair:
        copy.start()

    @pl.when(has_below)
    def _():
        lower[0].start()

    @pl.when(has_above)
    def _():
        raised[0].start()

    def spread(block, area, position):
        at = pl.ds(pl.multiple_of(area * span + position * rows, rows), rows)
        for w in range(half):
            for j in range(tiles):
                piece = block[w, :, j * LANES : (j + 1) * LANES]
                ext[w * tiles + j, at, :] = piece.astype(jnp.float32)

    def blank(area):
        at = pl.ds(area * span, span)
        ext[:, at, :] = jnp.zeros((half * tiles, span, LANES), jnp.float32)

    for w in range(half):
        pair[w].wait_recv()

        @pl.when(has_below)
        def _():
            lower[w + 1].start()

        @pl.when(has_above)
        def _():
            raised[w + 1].start()

    spread(keep, 1, y)
    spread(bufs.at[0], 1, 1 - y)

    @pl.when(has_above)
    def _():
        lower[0].wait_recv()
        spread(bufs.at[3], 2, y)
        for copy in lower[1:]:
            copy.wait_recv()
        spread(bufs.at[4], 2, 1 - y)

    @pl.when(jnp.logical_not(has_above))
    def _():
        blank(2)

    @pl.when(has_below)
    def _():
        raised[0].wait_recv()
        spread(bufs.at[1], 0, y)
        for copy in raised[1:]:
            copy.wait_recv()
        spread(bufs.at[2], 0, 1 - y)

    @pl.when(jnp.logical_not(has_below))
    def _():
        blank(0)

    def one_offset(owner, place_in):
        distance = offsets[owner * group + place_in]
        own = span - lax.div(distance, 2)

        def one_chunk(step, carry):
            at_a = pl.ds(own + step * chunk, chunk)
            at_b = pl.ds(own + distance + step * chunk, chunk)
            at = pl.ds(pl.multiple_of(step * chunk, chunk), chunk)
            for j in range(tiles // 2):
                real_sum = jnp.zeros((chunk, LANES), jnp.float32)
                imag_sum = jnp.zeros((chunk, LANES), jnp.float32)
                for w in range(half):
                    a_re = ext[w * tiles + j, at_a, :]
                    a_im = ext[w * tiles + tiles // 2 + j, at_a, :]
                    b_re = ext[w * tiles + j, at_b, :]
                    b_im = ext[w * tiles + tiles // 2 + j, at_b, :]
                    real_sum += a_re * b_re + a_im * b_im
                    imag_sum += a_im * b_re - a_re * b_im
                stack[at, j * LANES : (j + 1) * LANES] = real_sum.astype(jnp.bfloat16)
                lo = width // 2 + j * LANES
                stack[at, lo : lo + LANES] = imag_sum.astype(jnp.bfloat16)
            return carry

        lax.fori_loop(0, span // chunk, one_chunk, 0)
        lagged = jnp.dot(stack[...], back[...], preferred_element_type=jnp.float32)
        for part in range(split):
            piece = lagged[:, part * cols : (part + 1) * cols]
            parts[owner * split + part, place_in] = piece.astype(jnp.bfloat16)

    copies = []
    for s in range(owners):
        owner = lax.rem(t + 1 + s, owners)

        def body(place_in, carry, owner=owner):
            one_offset(owner, place_in)
            return carry

        lax.fori_loop(0, group, body, 0)
        for part in range(split) if s < owners - 1 else (1 - y,):
            p = owner * split + part
            k = lax.rem(p - me + peers, peers)
            copy = pltpu.make_async_remote_copy(
                src_ref=parts.at[p],
                dst_ref=landed.at[k],
                send_sem=send_sems.at[k],
                recv_sem=recv_sems.at[k],
                device_id=place(p),
                device_id_type=MESH,
            )
            copy.start()
            copies.append(copy)
    for copy in copies:
        copy.wait_recv()
    value = parts[me].astype(jnp.float32)
    for k in range(1, peers):
        value += landed[k].astype(jnp.float32)
    total[:, :span, :] = value
    down[...] = value.astype(jnp.bfloat16)
    hop = pltpu.make_async_remote_copy(
        src_ref=down,
        dst_ref=above,
        send_sem=hop_sems.at[0],
        recv_sem=hop_sems.at[1],
        device_id={"tm": t, "chan": beneath},
        device_id_type=MESH,
    )
    hop.start()
    hop.wait_recv()
    inside = (d + split < chans).astype(jnp.float32)
    total[:, span:, :] = above[...].astype(jnp.float32) * inside
    for o in range(group):
        skip = lax.div(offsets[t * group + o], 2)
        mine[o] = total[o, pl.ds(skip + (1 - y) * rows, rows), :] * scale
    swap = pltpu.make_async_remote_copy(
        src_ref=mine,
        dst_ref=theirs,
        send_sem=swap_sems.at[0],
        recv_sem=swap_sems.at[1],
        device_id={"tm": t, "chan": base + 1 - y},
        device_id_type=MESH,
    )
    swap.start()
    swap.wait_recv()
    for o in range(group):
        skip = lax.div(offsets[t * group + o], 2)
        own = total[o, pl.ds(skip + y * rows, rows), :] * scale
        other = theirs[o]
        out[o, :, :cols] = jnp.where(y == 0, own, other)
        out[o, :, cols:] = jnp.where(y == 0, other, own)
    for copy in copies:
        copy.wait_send()
    hop.wait_send()
    swap.wait_send()
    for copy in pair:
        copy.wait_send()

    @pl.when(has_below)
    def _():
        for copy in lower:
            copy.wait_send()

    @pl.when(has_above)
    def _():
        for copy in raised:
            copy.wait_send()


def cross(offsets, keep, give, back, owners, chans, split, scale):
    half, rows, width = keep.shape
    span = split * rows
    group = offsets.shape[0] // owners
    peers = owners * split
    cols = LAGS // split
    vmem = pl.BlockSpec(memory_space=pltpu.VMEM)
    return pl.pallas_call(
        functools.partial(cross_kernel, owners, chans, split, scale),
        out_shape=jax.ShapeDtypeStruct((group, rows, LAGS), jnp.float32),
        in_specs=[pl.BlockSpec(memory_space=pltpu.SMEM)] + [vmem] * 3,
        out_specs=vmem,
        scratch_shapes=[
            pltpu.VMEM((half * width // LANES, 3 * span, LANES), jnp.float32),
            pltpu.VMEM((span, width), jnp.bfloat16),
            pltpu.VMEM((peers, group, span, cols), jnp.bfloat16),
            pltpu.VMEM((peers, group, span, cols), jnp.bfloat16),
            pltpu.VMEM((group, 2 * span, cols), jnp.float32),
            pltpu.VMEM((group, span, cols), jnp.bfloat16),
            pltpu.VMEM((group, span, cols), jnp.bfloat16),
            pltpu.VMEM((group, rows, cols), jnp.float32),
            pltpu.VMEM((group, rows, cols), jnp.float32),
            pltpu.SemaphoreType.DMA((peers,)),
            pltpu.SemaphoreType.DMA((peers,)),
            pltpu.SemaphoreType.DMA((2,)),
            pltpu.SemaphoreType.DMA((2,)),
            pltpu.VMEM((5, half, rows, width), jnp.bfloat16),
            pltpu.SemaphoreType.DMA((3 * half + 2,)),
            pltpu.SemaphoreType.DMA((3 * half + 2,)),
        ],
        compiler_params=pltpu.CompilerParams(
            collective_id=0, has_side_effects=True, vmem_limit_bytes=40 * 2**20
        ),
        name="cross",
    )(offsets, keep, give, back)


def local(raw, starts, dead_mask, offsets):
    rows = raw.shape[0]
    window_count = starts.shape[0]
    owners = lax.axis_size("tm")
    chans = lax.axis_size("chan")
    split = MAXOFF // 2 // rows
    half = window_count // split
    halo = shifted(raw[:, :HOP], "tm", -1)
    live = dead_mask.astype(jnp.float32)[:, None]
    white = spectra(raw, halo, starts, live)
    y = lax.rem(lax.axis_index("chan"), split)
    keep = lax.dynamic_slice_in_dim(white, y * half, half, 0)
    give = lax.dynamic_slice_in_dim(white, (1 - y) * half, half, 0)
    back = inverse_table().astype(jnp.bfloat16)
    scale = float((window_count * owners * F) ** -0.5)
    return cross(offsets, keep, give, back, owners, chans, split, scale)


def solution(mesh):
    in_specs = (P("chan", "tm"), P("tm"), P("chan"), P())
    out_specs = P("tm", "chan", None)
    return jax.shard_map(local, mesh=mesh, in_specs=in_specs, out_specs=out_specs, check_vma=False)
```

```python
import functools

import jax
import jax.numpy as jnp
from jax import lax
from jax.experimental import pallas as pl
from jax.experimental.pallas import tpu as pltpu
from jax.sharding import PartitionSpec as P

HOP = 4096
F = 640
F0 = 16
LAGS = 256
MAXOFF = 256
LANES = 128
BLOCK = 512
FINE = 64
MESH = pl.DeviceIdType.MESH


def shifted(block, axis, distance):
    devices = range(lax.axis_size(axis))
    route = [(i - distance, i) for i in devices if i - distance in devices]
    return lax.ppermute(block, axis, route)


def waves(samples):
    bins = jnp.arange(F, dtype=jnp.int32) + F0
    phase = samples[:, None] * bins[None, :] % (2 * HOP)
    angle = 2.0 * jnp.pi / (2 * HOP) * phase.astype(jnp.float32)
    return jnp.cos(angle), jnp.sin(angle)


def base_table():
    fine_c, fine_s = waves(jnp.arange(FINE, dtype=jnp.int32))
    wide_c, wide_s = waves(jnp.arange(BLOCK // FINE, dtype=jnp.int32) * FINE)
    fine_c, fine_s = fine_c[None], fine_s[None]
    wide_c, wide_s = wide_c[:, None], wide_s[:, None]
    cosines = wide_c * fine_c - wide_s * fine_s
    sines = wide_s * fine_c + wide_c * fine_s
    return cosines.reshape(BLOCK, F), sines.reshape(BLOCK, F)


def inverse_table():
    lagged = jnp.arange(LAGS, dtype=jnp.int32) - LAGS // 2

    def turns(bins):
        phase = jnp.mod(bins[:, None] * lagged[None, :], 2 * HOP)
        angle = 2.0 * jnp.pi / (2 * HOP) * phase.astype(jnp.float32)
        return jnp.cos(angle), jnp.sin(angle)

    fine = 32
    fine_c, fine_s = turns(jnp.arange(fine, dtype=jnp.int32))
    wide_c, wide_s = turns(jnp.arange(F // fine, dtype=jnp.int32) * fine + F0)
    fine_c, fine_s = fine_c[None], fine_s[None]
    wide_c, wide_s = wide_c[:, None], wide_s[:, None]
    cosines = (wide_c * fine_c - wide_s * fine_s).reshape(F, LAGS)
    sines = (wide_s * fine_c + wide_c * fine_s).reshape(F, LAGS)
    return jnp.concatenate([cosines, -sines], axis=0)


def spectra_kernel(
    starts, raw, halo, base_c, base_s, turn_c, turn_s, hann, live, white, pad, tap, table,
    later_tap, later_table, acc, sems
):
    rows, length = raw.shape
    window_count = starts.shape[0]
    first = pltpu.make_async_copy(raw, pad.at[:, pl.ds(0, length)], sems.at[0])
    second = pltpu.make_async_copy(halo, pad.at[:, pl.ds(length, HOP)], sems.at[1])
    first.start()
    second.start()
    acc[...] = jnp.zeros_like(acc)
    lane = lax.broadcasted_iota(jnp.int32, (rows, LANES), 1)
    first.wait()
    second.wait()

    def prepare(number, tap, table):
        ct, st = turn_c[number], turn_s[number]
        bc, bs = base_c[...], base_s[...]
        table[:, :F] = (bc * ct - bs * st).astype(jnp.bfloat16)
        table[:, F:] = (-(bs * ct + bc * st)).astype(jnp.bfloat16)
        taper = hann[number]
        for w in range(window_count):
            begin = starts[w]
            rest = lax.rem(begin, LANES)
            column = pl.multiple_of(begin - rest + number * BLOCK, LANES)
            turn = lax.rem(LANES - rest, LANES)
            keep = lane < LANES - rest
            rolled = None
            for j in range(BLOCK // LANES + 1):
                piece = pad[:, pl.ds(pl.multiple_of(column + j * LANES, LANES), LANES)]
                following = pltpu.roll(piece.astype(jnp.float32), turn, 1)
                if j:
                    lo = (j - 1) * LANES
                    value = jnp.where(keep, rolled, following) * taper[:, lo : lo + LANES]
                    tap[w * rows : (w + 1) * rows, lo : lo + LANES] = value.astype(jnp.bfloat16)
                rolled = following

    blocks = 2 * HOP // BLOCK
    prepare(0, tap, table)

    def step(number, carry):
        prepare(2 * number + 1, later_tap, later_table)
        acc[...] += jnp.dot(tap[...], table[...], preferred_element_type=jnp.float32)
        prepare(lax.rem(2 * number + 2, blocks), tap, table)
        acc[...] += jnp.dot(later_tap[...], later_table[...], preferred_element_type=jnp.float32)
        return carry

    lax.fori_loop(0, blocks // 2, step, 0)

    def whiten(w, carry):
        at = pl.ds(pl.multiple_of(w * rows, rows), rows)
        real_part = acc[at, :F]
        imag_part = acc[at, F:]
        amplitude = jnp.sqrt(real_part * real_part + imag_part * imag_part)
        level = jnp.mean(amplitude, axis=-1, keepdims=True)
        scaled = live[...] / (amplitude + 0.1 * level + 1e-06)
        white[w, :, :F] = (real_part * scaled).astype(jnp.bfloat16)
        white[w, :, F:] = (imag_part * scaled).astype(jnp.bfloat16)
        return carry

    lax.fori_loop(0, window_count, whiten, 0)


def spectra(raw, halo, starts, live):
    rows, length = raw.shape
    window_count = starts.shape[0]
    blocks = 2 * HOP // BLOCK
    base_c, base_s = base_table()
    turn_c, turn_s = waves(jnp.arange(blocks, dtype=jnp.int32) * BLOCK)
    sample = jnp.arange(2 * HOP, dtype=jnp.float32)
    hann = 0.5 - 0.5 * jnp.cos(2.0 * jnp.pi * sample / (2 * HOP))
    vmem = pl.BlockSpec(memory_space=pltpu.VMEM)
    hbm = pl.BlockSpec(memory_space=pl.ANY)
    total = window_count * rows
    return pl.pallas_call(
        spectra_kernel,
        out_shape=jax.ShapeDtypeStruct((window_count, rows, 2 * F), jnp.bfloat16),
        in_specs=[pl.BlockSpec(memory_space=pltpu.SMEM), hbm, hbm] + [vmem] * 6,
        out_specs=vmem,
        scratch_shapes=[
            pltpu.VMEM((rows, length + HOP + LANES), jnp.bfloat16),
            pltpu.VMEM((total, BLOCK), jnp.bfloat16),
            pltpu.VMEM((BLOCK, 2 * F), jnp.bfloat16),
            pltpu.VMEM((total, BLOCK), jnp.bfloat16),
            pltpu.VMEM((BLOCK, 2 * F), jnp.bfloat16),
            pltpu.VMEM((total, 2 * F), jnp.float32),
            pltpu.SemaphoreType.DMA((2,)),
        ],
        compiler_params=pltpu.CompilerParams(vmem_limit_bytes=48 * 2**20),
        name="spectra",
    )(
        starts, raw, halo, base_c, base_s,
        turn_c.reshape(blocks, 1, F), turn_s.reshape(blocks, 1, F),
        hann.reshape(blocks, 1, BLOCK), live,
    )


def cross_kernel(owners, chans, split, scale, offsets, *refs):
    (keep, give, back, out, ext, stack, parts, landed, total, down, above, mine, theirs,
     send_sems, recv_sems, hop_sems, swap_sems, bufs, out_sems, in_sems) = refs
    half, rows, width = keep.shape
    span = split * rows
    tiles = width // LANES
    peers, group, _, cols = parts.shape
    chunk = 16
    t = lax.axis_index("tm")
    d = lax.axis_index("chan")
    y = lax.rem(d, split)
    base = d - y
    me = t * split + y
    beneath = lax.rem(d - split + chans, chans)
    upper = lax.rem(d + split, chans)

    def place(p):
        return {"tm": lax.div(p, split), "chan": base + lax.rem(p, split)}

    barrier = pltpu.get_barrier_semaphore()
    for k in range(1, peers):
        pl.semaphore_signal(
            barrier, inc=1, device_id=place(lax.rem(me + k, peers)), device_id_type=MESH
        )
    for c in (beneath, upper):
        pl.semaphore_signal(
            barrier, inc=1, device_id={"tm": t, "chan": c}, device_id_type=MESH
        )

    pl.semaphore_wait(barrier, peers + 1)

    def remote(src, dst, number, chan):
        return pltpu.make_async_remote_copy(
            src_ref=src,
            dst_ref=dst,
            send_sem=out_sems.at[number],
            recv_sem=in_sems.at[number],
            device_id={"tm": t, "chan": chan},
            device_id_type=MESH,
        )

    partner = base + 1 - y
    pair = [remote(give.at[w], bufs.at[0, w], w, partner) for w in range(half)]
    lower = [remote(keep, bufs.at[3], half, beneath)]
    raised = [remote(keep, bufs.at[1], half + 1, upper)]
    for w in range(half):
        lower.append(remote(bufs.at[0, w], bufs.at[4, w], half + 2 + w, beneath))
        raised.append(remote(bufs.at[0, w], bufs.at[2, w], 2 * half + 2 + w, upper))
    has_below = d >= split
    has_above = d + split < chans

    for copy in pair:
        copy.start()

    @pl.when(has_below)
    def _():
        lower[0].start()

    @pl.when(has_above)
    def _():
        raised[0].start()

    def spread(block, area, position, windows=range(half)):
        at = pl.ds(pl.multiple_of(area * span + position * rows, rows), rows)
        for w in windows:
            for j in range(tiles):
                piece = block[w, :, j * LANES : (j + 1) * LANES]
                ext[w * tiles + j, at, :] = piece.astype(jnp.float32)

    def blank(area):
        at = pl.ds(area * span, span)
        ext[:, at, :] = jnp.zeros((half * tiles, span, LANES), jnp.float32)

    for w in range(half):
        pair[w].wait_recv()

        @pl.when(has_below)
        def _():
            lower[w + 1].start()

        @pl.when(has_above)
        def _():
            raised[w + 1].start()

    spread(keep, 1, y)
    spread(bufs.at[0], 1, 1 - y)

    @pl.when(has_above)
    def _():
        lower[0].wait_recv()
        spread(bufs.at[3], 2, y)

    @pl.when(jnp.logical_not(has_above))
    def _():
        blank(2)

    @pl.when(has_below)
    def _():
        raised[0].wait_recv()
        spread(bufs.at[1], 0, y)

    @pl.when(jnp.logical_not(has_below))
    def _():
        blank(0)

    for w in range(half):

        @pl.when(has_above)
        def _():
            lower[w + 1].wait_recv()
            spread(bufs.at[4], 2, 1 - y, (w,))

        @pl.when(has_below)
        def _():
            raised[w + 1].wait_recv()
            spread(bufs.at[2], 0, 1 - y, (w,))

    def one_offset(owner, place_in):
        distance = offsets[owner * group + place_in]
        own = span - lax.div(distance, 2)

        def one_chunk(step, carry):
            at_a = pl.ds(own + step * chunk, chunk)
            at_b = pl.ds(own + distance + step * chunk, chunk)
            at = pl.ds(pl.multiple_of(step * chunk, chunk), chunk)
            for j in range(tiles // 2):
                real_sum = jnp.zeros((chunk, LANES), jnp.float32)
                imag_sum = jnp.zeros((chunk, LANES), jnp.float32)
                for w in range(half):
                    a_re = ext[w * tiles + j, at_a, :]
                    a_im = ext[w * tiles + tiles // 2 + j, at_a, :]
                    b_re = ext[w * tiles + j, at_b, :]
                    b_im = ext[w * tiles + tiles // 2 + j, at_b, :]
                    real_sum += a_re * b_re + a_im * b_im
                    imag_sum += a_im * b_re - a_re * b_im
                stack[at, j * LANES : (j + 1) * LANES] = real_sum.astype(jnp.bfloat16)
                lo = width // 2 + j * LANES
                stack[at, lo : lo + LANES] = imag_sum.astype(jnp.bfloat16)
            return carry

        lax.fori_loop(0, span // chunk, one_chunk, 0)
        lagged = jnp.dot(stack[...], back[...], preferred_element_type=jnp.float32)
        for part in range(split):
            piece = lagged[:, part * cols : (part + 1) * cols]
            parts[owner * split + part, place_in] = piece.astype(jnp.bfloat16)

    copies = []
    for s in range(owners):
        owner = lax.rem(t + 1 + s, owners)

        def body(place_in, carry, owner=owner):
            one_offset(owner, place_in)
            return carry

        lax.fori_loop(0, group, body, 0)
        for part in range(split) if s < owners - 1 else (1 - y,):
            p = owner * split + part
            k = lax.rem(p - me + peers, peers)
            copy = pltpu.make_async_remote_copy(
                src_ref=parts.at[p],
                dst_ref=landed.at[k],
                send_sem=send_sems.at[k],
                recv_sem=recv_sems.at[k],
                device_id=place(p),
                device_id_type=MESH,
            )
            copy.start()
            copies.append(copy)
    for copy in copies:
        copy.wait_recv()
    value = parts[me].astype(jnp.float32)
    for k in range(1, peers):
        value += landed[k].astype(jnp.float32)
    total[:, :span, :] = value
    down[...] = value.astype(jnp.bfloat16)
    hop = pltpu.make_async_remote_copy(
        src_ref=down,
        dst_ref=above,
        send_sem=hop_sems.at[0],
        recv_sem=hop_sems.at[1],
        device_id={"tm": t, "chan": beneath},
        device_id_type=MESH,
    )
    hop.start()
    hop.wait_recv()
    inside = (d + split < chans).astype(jnp.float32)
    total[:, span:, :] = above[...].astype(jnp.float32) * inside
    for o in range(group):
        skip = lax.div(offsets[t * group + o], 2)
        mine[o] = total[o, pl.ds(skip + (1 - y) * rows, rows), :] * scale
    swap = pltpu.make_async_remote_copy(
        src_ref=mine,
        dst_ref=theirs,
        send_sem=swap_sems.at[0],
        recv_sem=swap_sems.at[1],
        device_id={"tm": t, "chan": base + 1 - y},
        device_id_type=MESH,
    )
    swap.start()
    swap.wait_recv()
    for o in range(group):
        skip = lax.div(offsets[t * group + o], 2)
        own = total[o, pl.ds(skip + y * rows, rows), :] * scale
        other = theirs[o]
        out[o, :, :cols] = jnp.where(y == 0, own, other)
        out[o, :, cols:] = jnp.where(y == 0, other, own)
    for copy in copies:
        copy.wait_send()
    hop.wait_send()
    swap.wait_send()
    for copy in pair:
        copy.wait_send()

    @pl.when(has_below)
    def _():
        for copy in lower:
            copy.wait_send()

    @pl.when(has_above)
    def _():
        for copy in raised:
            copy.wait_send()


def cross(offsets, keep, give, back, owners, chans, split, scale):
    half, rows, width = keep.shape
    span = split * rows
    group = offsets.shape[0] // owners
    peers = owners * split
    cols = LAGS // split
    vmem = pl.BlockSpec(memory_space=pltpu.VMEM)
    return pl.pallas_call(
        functools.partial(cross_kernel, owners, chans, split, scale),
        out_shape=jax.ShapeDtypeStruct((group, rows, LAGS), jnp.float32),
        in_specs=[pl.BlockSpec(memory_space=pltpu.SMEM)] + [vmem] * 3,
        out_specs=vmem,
        scratch_shapes=[
            pltpu.VMEM((half * width // LANES, 3 * span, LANES), jnp.float32),
            pltpu.VMEM((span, width), jnp.bfloat16),
            pltpu.VMEM((peers, group, span, cols), jnp.bfloat16),
            pltpu.VMEM((peers, group, span, cols), jnp.bfloat16),
            pltpu.VMEM((group, 2 * span, cols), jnp.float32),
            pltpu.VMEM((group, span, cols), jnp.bfloat16),
            pltpu.VMEM((group, span, cols), jnp.bfloat16),
            pltpu.VMEM((group, rows, cols), jnp.float32),
            pltpu.VMEM((group, rows, cols), jnp.float32),
            pltpu.SemaphoreType.DMA((peers,)),
            pltpu.SemaphoreType.DMA((peers,)),
            pltpu.SemaphoreType.DMA((2,)),
            pltpu.SemaphoreType.DMA((2,)),
            pltpu.VMEM((5, half, rows, width), jnp.bfloat16),
            pltpu.SemaphoreType.DMA((3 * half + 2,)),
            pltpu.SemaphoreType.DMA((3 * half + 2,)),
        ],
        compiler_params=pltpu.CompilerParams(
            collective_id=0, has_side_effects=True, vmem_limit_bytes=40 * 2**20
        ),
        name="cross",
    )(offsets, keep, give, back)


def local(raw, starts, dead_mask, offsets):
    rows = raw.shape[0]
    window_count = starts.shape[0]
    owners = lax.axis_size("tm")
    chans = lax.axis_size("chan")
    split = MAXOFF // 2 // rows
    half = window_count // split
    halo = shifted(raw[:, :HOP], "tm", -1)
    live = dead_mask.astype(jnp.float32)[:, None]
    white = spectra(raw, halo, starts, live)
    y = lax.rem(lax.axis_index("chan"), split)
    keep = lax.dynamic_slice_in_dim(white, y * half, half, 0)
    give = lax.dynamic_slice_in_dim(white, (1 - y) * half, half, 0)
    back = inverse_table().astype(jnp.bfloat16)
    scale = float((window_count * owners * F) ** -0.5)
    return cross(offsets, keep, give, back, owners, chans, split, scale)


def solution(mesh):
    in_specs = (P("chan", "tm"), P("tm"), P("chan"), P())
    out_specs = P("tm", "chan", None)
    return jax.shard_map(local, mesh=mesh, in_specs=in_specs, out_specs=out_specs, check_vma=False)
```
